256 devices in a mesh: section: 8 (over x, z_lo), dp: 32 (over z_hi, y, core).
Axes of the slice: x: 4, y: 4, z: 8 (z_hi: 4, z_lo: 2; z = z_hi * 2 + z_lo), core: 2. Of those that a mesh axis runs over, the one named last changes fastest.
Arguments:
- enc_in: bfloat16 [512, 16, 16, 320], P(('dp', 'section')), parts along dimension 0, may hold values from -6 to 6
- dec_in: bfloat16 [512, 16, 16, 320], P(('dp', 'section')), parts along dimension 0, may hold values from -6 to 6
- fresh: bfloat16 [64, 16, 16, 320], P('dp'), parts along dimension 0, may hold values from -6 to 6
- skip_queue: bfloat16 [1024, 16, 16, 320], P(('dp', 'section')), parts along dimension 0, may hold values from -6 to 6
- enc_weight: bfloat16 [8, 3, 3, 320, 320], P('section'), may hold values from -0.109375 to 0.109375
- enc_bias: float32 [8, 320], P('section'), may hold values from -2 to 2
- enc_gain: float32 [8, 320], P('section'), may hold values from 0.25 to 1.75
- enc_beta: float32 [8, 320], P('section'), may hold values from -2 to 2
- dec_weight: bfloat16 [8, 3, 3, 640, 320], P('section'), may hold values from -0.078125 to 0.078125
- dec_bias: float32 [8, 320], P('section'), may hold values from -2 to 2
- dec_gain: float32 [8, 640], P('section'), may hold values from 0.25 to 1.75
- dec_beta: float32 [8, 640], P('section'), may hold values from -2 to 2
Outputs:
- encoded: bfloat16 [1024, 16, 16, 320], P(('dp', 'section')), parts along dimension 0
- decoded: bfloat16 [1024, 16, 16, 320], P(('dp', 'section')), parts along dimension 0
- queued: bfloat16 [1024, 16, 16, 320], P(('dp', 'section')), parts along dimension 0
The draws below stay inside these ranges and needn't reach their ends.
There are 32 independent parts, one for each index of `dp`. The reference program is written for one: setup_inputs(seed, part) draws one part's arguments, and reference() takes and returns one part's arrays. A program takes and returns all parts, laid end to end along the dimension named above; an argument that names none is the same for every part. Nothing has to cross between parts.
All inputs are finite; a program needn't handle non-finite values.
Results may differ from the reference program's by a relative error of at most 0.0048.
Values may be sent and summed in bfloat16 or wider, within the bound.
No kernel may reach another device: no remote copies, remote signals or barrier semaphores. Data moves between devices by JAX's collectives and lax.ppermute only.
A program may use at most 64 MiB of HBM per device.

```python
import jax
import jax.numpy as jnp
from jax import lax

C = 320
GROUPS = 32
SIDE = 16
TICKS = 2
IMG = 2
N_SECTION = 8


def block_scale(stream_key, shape, shards, least, high):
    def one(axis_at, blocks):
        heights = jax.random.uniform(jax.random.fold_in(jax.random.fold_in(stream_key, 6), axis_at), (blocks,), jnp.float32, least / len(shards), high / len(shards))
        return jnp.repeat(jnp.exp(heights), shape[axis_at] // blocks).reshape((-1,) + (1,) * (len(shape) - axis_at - 1))

    gain = one(*shards[0])
    for cut in shards[1:]:
        gain = gain * one(*cut)
    return gain


def noise(rng, dims, deviation, bound, cuts=(), kind=jnp.bfloat16):
    level = block_scale(rng, dims, cuts, -0.22, 0.18) if cuts else 1.0
    drawn = jax.random.normal(rng, dims, jnp.float32) * deviation * level
    return jnp.minimum(jnp.maximum(drawn, -bound), bound).astype(kind)


def setup_inputs(seed: int = 0, part: int = 0) -> dict:
    keys = jax.random.split(jax.random.key(seed), 13)
    part_splits = jax.random.split(jax.random.fold_in(keys[12], part), 13)
    enc_in = noise(part_splits[0], (N_SECTION * IMG, SIDE, SIDE, C), 1.0, 6.0, ((0, 8),))
    dec_in = noise(part_splits[1], (N_SECTION * IMG, SIDE, SIDE, C), 1.0, 6.0, ((0, 8),))
    fresh = noise(part_splits[2], ((TICKS - 1) * IMG, SIDE, SIDE, C), 1.0, 6.0)
    skip_queue = noise(part_splits[3], (N_SECTION * TICKS * IMG, SIDE, SIDE, C), 1.0, 6.0, ((0, 8),))
    enc_weight = noise(keys[4], (N_SECTION, 3, 3, C, C), (9 * C) ** -0.5, 0.109375, ((0, 8),))
    enc_bias = noise(keys[5], (N_SECTION, C), 0.3, 2.0, ((0, 8),), jnp.float32)
    enc_gain = jnp.clip(1.0 + 0.15 * jax.random.normal(keys[6], (N_SECTION, C), jnp.float32), 0.25, 1.75)
    enc_beta = noise(keys[7], (N_SECTION, C), 0.3, 2.0, ((0, 8),), jnp.float32)
    dec_weight = noise(keys[8], (N_SECTION, 3, 3, 2 * C, C), (18 * C) ** -0.5, 0.078125, ((0, 8),))
    dec_bias = noise(keys[9], (N_SECTION, C), 0.3, 2.0, ((0, 8),), jnp.float32)
    dec_gain = jnp.clip(1.0 + 0.15 * jax.random.normal(keys[10], (N_SECTION, 2 * C), jnp.float32), 0.25, 1.75)
    dec_beta = noise(keys[11], (N_SECTION, 2 * C), 0.3, 2.0, ((0, 8),), jnp.float32)
    return dict(enc_in=enc_in, dec_in=dec_in, fresh=fresh, skip_queue=skip_queue, enc_weight=enc_weight, enc_bias=enc_bias, enc_gain=enc_gain, enc_beta=enc_beta, dec_weight=dec_weight, dec_bias=dec_bias, dec_gain=dec_gain, dec_beta=dec_beta)


def norm_silu(values, norm_gain, norm_beta):
    layout = values.shape
    grouped = values.reshape(layout[:3] + (GROUPS, layout[3] // GROUPS))
    average = lax.optimization_barrier(jnp.mean(grouped, axis=(1, 2, 4), keepdims=True))
    centred = grouped - average
    variance = lax.optimization_barrier(jnp.mean(centred * centred, axis=(1, 2, 4), keepdims=True))
    normed = (centred * lax.rsqrt(variance + 1e-05)).reshape(layout)
    return jax.nn.silu(normed * norm_gain + norm_beta).astype(jnp.bfloat16)

def convolve(inputs, kernel):
    return lax.conv_general_dilated(inputs, kernel, (1, 1), 'SAME', dimension_numbers=('NHWC', 'HWIO', 'NHWC'), preferred_element_type=jnp.float32)

def encode(current, kernel, bias_row, norm_gain, norm_beta):
    widened = current.astype(jnp.float32)
    hidden = norm_silu(widened, norm_gain, norm_beta)
    return (widened + convolve(hidden, kernel) + bias_row).astype(jnp.bfloat16)

def decode(current, skipped, kernel, bias_row, norm_gain, norm_beta):
    joined = jnp.concatenate([current, skipped], axis=3).astype(jnp.float32)
    hidden = norm_silu(joined, norm_gain, norm_beta)
    return (current.astype(jnp.float32) + convolve(hidden, kernel) + bias_row).astype(jnp.bfloat16)

def reference(enc_in, dec_in, fresh, skip_queue, enc_weight, enc_bias, enc_gain, enc_beta, dec_weight, dec_bias, dec_gain, dec_beta):
    sections = N_SECTION
    map_dims = enc_in.shape[1:]
    images = enc_in.shape[0] // sections
    enc_now = enc_in.reshape((sections, images) + map_dims)
    dec_now = dec_in.reshape((sections, images) + map_dims)
    queue = skip_queue.reshape((sections, TICKS, images) + map_dims)
    arrivals = fresh.reshape((TICKS - 1, images) + map_dims)
    enc_list, dec_list, queue_list = ([], [], [])
    previous = None
    for turn_index in range(TICKS):
        skipped = queue[:, turn_index]
        if turn_index > 0:
            skipped = skipped.at[0].set(previous)
        enc_out = jax.vmap(encode)(enc_now, enc_weight, enc_bias, enc_gain, enc_beta)
        dec_out = jax.vmap(decode)(dec_now, skipped, dec_weight, dec_bias, dec_gain, dec_beta)
        received = enc_out[::-1]
        previous = received[0]
        enc_list.append(enc_out)
        dec_list.append(dec_out)
        queue_list.append(received)
        if turn_index + 1 < TICKS:
            enc_now = jnp.concatenate([arrivals[turn_index][None], enc_out[:-1]], axis=0)
            dec_now = jnp.concatenate([enc_out[-1:], dec_out[:-1]], axis=0)
    whole = (sections * TICKS * images,) + map_dims
    encoded = jnp.stack(enc_list, axis=1).reshape(whole)
    decoded = jnp.stack(dec_list, axis=1).reshape(whole)
    queued = jnp.stack(queue_list, axis=1).reshape(whole)
    return (encoded, decoded, queued)
```

```python
import jax
import jax.numpy as jnp
from jax import lax
from jax.experimental import pallas as pl
from jax.experimental.pallas import tpu as pltpu
from jax.sharding import PartitionSpec as P

GROUPS = 32
TICKS = 2
IMAGES = 2
SIDE = 16
CELLS = SIDE * SIDE
HALF = CELLS // 2
C = 320
ROWS = IMAGES * CELLS
TAPS = 3 * C
F32 = jnp.float32
BF16 = jnp.bfloat16
ANY = pl.BlockSpec(memory_space=pl.ANY)
VMEM = pl.BlockSpec(memory_space=pltpu.VMEM)
SMEM = pl.BlockSpec(memory_space=pltpu.SMEM)


def group_matrix(width):
    scale = 65536 // width + 1
    rows = lax.shift_right_logical(lax.broadcasted_iota(jnp.int32, (C, C), 0) * scale, 16)
    cols = lax.shift_right_logical(lax.broadcasted_iota(jnp.int32, (C, C), 1) * scale, 16)
    return jnp.where(rows == cols, 1.0, 0.0).astype(BF16)


def column_parts(values):
    return jnp.sum(values.reshape(CELLS // 8, 8, C), axis=0)


def group_means(parts, matrix, width):
    pieces = []
    for part in parts:
        high = part.astype(BF16).astype(F32)
        rest = part - high
        middle = rest.astype(BF16).astype(F32)
        pieces += [high, middle, rest - middle]
    stacked = jnp.concatenate(pieces, axis=0).astype(BF16)
    sums = jnp.dot(stacked, matrix, preferred_element_type=F32)
    weight = 1.0 / (width * CELLS)
    return [jnp.sum(sums[24 * i : 24 * (i + 1)], axis=0, keepdims=True) * weight for i in range(len(parts))]


def norm_all(loads, gains, betas, width):
    matrix = group_matrix(width)
    means = group_means([column_parts(load().astype(F32)) for load in loads], matrix, width)
    squares = []
    for load, mean in zip(loads, means):
        centred = load().astype(F32) - mean
        squares.append(column_parts(centred * centred))
    variances = group_means(squares, matrix, width)
    results = []
    for load, mean, variance, gain, beta in zip(loads, means, variances, gains, betas):
        half = ((load().astype(F32) - mean) * (lax.rsqrt(variance + 1e-05) * gain) + beta) * 0.5
        results.append((half * jnp.tanh(half) + half).astype(BF16))
    return results


def spread_rows(hidden):
    blank = jnp.zeros((SIDE, C), BF16)
    above = jnp.concatenate([blank, hidden[: CELLS - SIDE]], axis=0)
    below = jnp.concatenate([hidden[SIDE:], blank], axis=0)
    return jnp.concatenate([above, hidden, below], axis=1)


def gather_columns(sums):
    column = lax.broadcasted_iota(jnp.int32, (CELLS, C), 0) & (SIDE - 1)
    left = jnp.where(column > 0, pltpu.roll(sums[:, :C], 1, 0), 0.0)
    right = jnp.where(column < SIDE - 1, pltpu.roll(sums[:, 2 * C :], CELLS - 1, 0), 0.0)
    return left + sums[:, C : 2 * C] + right


def pack(value):
    return jnp.concatenate([value[:HALF], value[HALF:]], axis=1)


def unpack(value):
    return jnp.concatenate([value[:, :C], value[:, C:]], axis=0)


def copy_in(source, target, semaphore):
    copy = pltpu.make_async_copy(source, target, semaphore)
    copy.start()
    return copy


def make_enc(turn):
    def body(*refs):
        if turn == 0:
            source, weight, bias, gain, beta, out, send, *scratch = refs
        else:
            place, fresh, received, _, weight, bias, gain, beta, out, send, *scratch = refs
        current, kernel, taps, wide, sums, result, sems = scratch
        weight_copy = copy_in(weight, kernel, sems.at[0])
        if turn == 0:
            copy_in(source, current, sems.at[1]).wait()
        else:
            leading = place[0] == 0

            @pl.when(leading)
            def _():
                copy_in(fresh, current, sems.at[1]).wait()

            @pl.when(jnp.logical_not(leading))
            def _():
                for i in range(IMAGES):
                    current[pl.ds(i * CELLS, CELLS)] = unpack(received[i])

        loads = [lambda i=i: current[pl.ds(i * CELLS, CELLS)] for i in range(IMAGES)]
        hidden = norm_all(loads, [gain[...]] * IMAGES, [beta[...]] * IMAGES, C // GROUPS)
        for i in range(IMAGES):
            wide[pl.ds(i * CELLS, CELLS)] = spread_rows(hidden[i])
        weight_copy.wait()
        for ky in range(3):
            taps[pl.ds(ky * C, C)] = jnp.concatenate([kernel[ky, kx] for kx in range(3)], axis=1)
        sums[...] = jnp.dot(wide[...], taps[...], preferred_element_type=F32)
        copies = []
        for i in range(IMAGES):
            rows = pl.ds(i * CELLS, CELLS)
            total = (current[rows].astype(F32) + gather_columns(sums[rows]) + bias[...]).astype(BF16)
            result[rows] = total
            send[i] = pack(total)
            copies.append(copy_in(result.at[rows], out.at[pl.ds(turn * ROWS + i * CELLS, CELLS)], sems.at[2 + i]))
        for copy in copies:
            copy.wait()

    scratch = [
        pltpu.VMEM((ROWS, C), BF16),
        pltpu.VMEM((3, 3, C, C), BF16),
        pltpu.VMEM((TAPS, TAPS), BF16),
        pltpu.VMEM((ROWS, TAPS), BF16),
        pltpu.VMEM((ROWS, TAPS), F32),
        pltpu.VMEM((ROWS, C), BF16),
        pltpu.SemaphoreType.DMA((4,)),
    ]
    out_shape = (
        jax.ShapeDtypeStruct((TICKS * ROWS, C), BF16),
        jax.ShapeDtypeStruct((IMAGES, HALF, 2 * C), BF16),
    )
    if turn == 0:
        return pl.pallas_call(
            body,
            out_shape=out_shape,
            in_specs=[ANY, ANY, VMEM, VMEM, VMEM],
            out_specs=(ANY, VMEM),
            scratch_shapes=scratch,
            name="enc_first",
        )
    return pl.pallas_call(
        body,
        out_shape=out_shape,
        in_specs=[SMEM, ANY, VMEM, ANY, ANY, VMEM, VMEM, VMEM],
        out_specs=(ANY, VMEM),
        scratch_shapes=scratch,
        input_output_aliases={3: 0},
        name="enc_second",
    )


def make_dec(turn):
    def body(*refs):
        if turn == 0:
            source, skips, weight, bias, gain, beta, out, send, *scratch = refs
        else:
            place, received_enc, received_dec, skips, _, weight, bias, gain, beta, out, *scratch = refs
        current, skipped, kernel, taps, wide, sums, result, sems = scratch
        weight_copy = copy_in(weight, kernel, sems.at[0])
        if turn == 0:
            first = copy_in(source, current, sems.at[1])
            second = copy_in(skips.at[pl.ds(0, ROWS)], skipped, sems.at[2])
            first.wait()
            second.wait()
        else:
            leading = place[0] == 0

            @pl.when(leading)
            def _():
                for i in range(IMAGES):
                    rows = pl.ds(i * CELLS, CELLS)
                    value = unpack(received_enc[i])
                    skipped[rows] = value
                    current[rows] = value

            @pl.when(jnp.logical_not(leading))
            def _():
                second = copy_in(skips.at[pl.ds(ROWS, ROWS)], skipped, sems.at[2])
                for i in range(IMAGES):
                    current[pl.ds(i * CELLS, CELLS)] = unpack(received_dec[i])
                second.wait()

        maps = (current, skipped)
        loads = [lambda m=m, i=i: m[pl.ds(i * CELLS, CELLS)] for m in maps for i in range(IMAGES)]
        gains = [gain[:, :C]] * IMAGES + [gain[:, C:]] * IMAGES
        betas = [beta[:, :C]] * IMAGES + [beta[:, C:]] * IMAGES
        hidden = norm_all(loads, gains, betas, 2 * C // GROUPS)
        for i in range(IMAGES):
            rows = pl.ds(i * CELLS, CELLS)
            wide[rows, :TAPS] = spread_rows(hidden[i])
            wide[rows, TAPS:] = spread_rows(hidden[IMAGES + i])
        weight_copy.wait()
        taps[:, :TAPS] = jnp.concatenate([kernel[ky, :, :C] for ky in range(3)], axis=1)
        taps[:, TAPS:] = jnp.concatenate([kernel[ky, :, C:] for ky in range(3)], axis=1)
        sums[...] = lax.dot_general(wide[...], taps[...], (((1,), (1,)), ((), ())), preferred_element_type=F32)
        copies = []
        for i in range(IMAGES):
            rows = pl.ds(i * CELLS, CELLS)
            total = (current[rows].astype(F32) + gather_columns(sums[rows]) + bias[...]).astype(BF16)
            if turn == 0:
                send[i] = pack(total)
            result[rows] = total
            copies.append(copy_in(result.at[rows], out.at[pl.ds(turn * ROWS + i * CELLS, CELLS)], sems.at[3 + i]))
        for copy in copies:
            copy.wait()

    scratch = [
        pltpu.VMEM((ROWS, C), BF16),
        pltpu.VMEM((ROWS, C), BF16),
        pltpu.VMEM((3, TAPS, 2 * C), BF16),
        pltpu.VMEM((TAPS, 2 * TAPS), BF16),
        pltpu.VMEM((ROWS, 2 * TAPS), BF16),
        pltpu.VMEM((ROWS, TAPS), F32),
        pltpu.VMEM((ROWS, C), BF16),
        pltpu.SemaphoreType.DMA((5,)),
    ]
    whole = jax.ShapeDtypeStruct((TICKS * ROWS, C), BF16)
    if turn == 0:
        return pl.pallas_call(
            body,
            out_shape=(whole, jax.ShapeDtypeStruct((IMAGES, HALF, 2 * C), BF16)),
            in_specs=[ANY, ANY, ANY, VMEM, VMEM, VMEM],
            out_specs=(ANY, VMEM),
            scratch_shapes=scratch,
            name="dec_first",
        )
    return pl.pallas_call(
        body,
        out_shape=whole,
        in_specs=[SMEM, VMEM, VMEM, ANY, ANY, ANY, VMEM, VMEM, VMEM],
        out_specs=ANY,
        scratch_shapes=scratch,
        input_output_aliases={4: 0},
        name="dec_second",
    )


def make_queue(turn):
    def body(*refs):
        if turn == 0:
            place, direct, shifted, out, result, sems = refs
            shared = jnp.logical_or(place[0] == 0, place[0] == 4)
        else:
            direct, _, out, result, sems = refs
        copies = []
        for i in range(IMAGES):
            value = direct[i]
            if turn == 0:
                value = jnp.where(shared, shifted[i], value)
            rows = pl.ds(i * CELLS, CELLS)
            result[rows] = unpack(value)
            copies.append(copy_in(result.at[rows], out.at[pl.ds(turn * ROWS + i * CELLS, CELLS)], sems.at[i]))
        for copy in copies:
            copy.wait()

    return pl.pallas_call(
        body,
        out_shape=jax.ShapeDtypeStruct((TICKS * ROWS, C), BF16),
        in_specs=[SMEM, VMEM, VMEM] if turn == 0 else [VMEM, ANY],
        out_specs=ANY,
        scratch_shapes=[pltpu.VMEM((ROWS, C), BF16), pltpu.SemaphoreType.DMA((IMAGES,))],
        input_output_aliases={} if turn == 0 else {1: 0},
        name="queue_first" if turn == 0 else "queue_second",
    )


def shards(
    enc_in,
    dec_in,
    fresh,
    skip_queue,
    enc_weight,
    enc_bias,
    enc_gain,
    enc_beta,
    dec_weight,
    dec_bias,
    dec_gain,
    dec_beta,
):
    place = lax.axis_index("section").astype(jnp.int32).reshape(1)
    forward = [(s, (s + 1) % 8) for s in range(8)]
    mirror = [(s, 7 - s) for s in range(8)]
    enc_kernel = enc_weight.reshape(3, 3, C, C)
    dec_kernel = jnp.transpose(dec_weight, (0, 1, 2, 4, 3)).reshape(3, TAPS, 2 * C)
    skips = skip_queue.reshape(TICKS * ROWS, C)

    encoded, enc_sent = make_enc(0)(enc_in.reshape(ROWS, C), enc_kernel, enc_bias, enc_gain, enc_beta)
    enc_moved = lax.ppermute(enc_sent, "section", forward)
    decoded, dec_sent = make_dec(0)(dec_in.reshape(ROWS, C), skips, dec_kernel, dec_bias, dec_gain, dec_beta)
    dec_moved = lax.ppermute(dec_sent, "section", [pair for pair in forward if pair[1] != 0])
    enc_turned = lax.ppermute(enc_sent, "section", [pair for pair in mirror if pair[1] not in (0, 4)])
    encoded, last_sent = make_enc(1)(
        place, fresh.reshape(ROWS, C), enc_moved, encoded, enc_kernel, enc_bias, enc_gain, enc_beta
    )
    last_turned = lax.ppermute(last_sent, "section", mirror)
    decoded = make_dec(1)(
        place, enc_moved, dec_moved, skips, decoded, dec_kernel, dec_bias, dec_gain, dec_beta
    )
    queued = make_queue(0)(place, enc_turned, enc_moved)
    queued = make_queue(1)(last_turned, queued)
    shape = (TICKS * IMAGES, SIDE, SIDE, C)
    return encoded.reshape(shape), decoded.reshape(shape), queued.reshape(shape)


def solution(mesh):
    maps = P(("dp", "section"), None, None, None)
    rows = P("section", None)
    kernels = P("section", None, None, None, None)
    in_specs = (maps, maps, P("dp", None, None, None), maps) + (kernels, rows, rows, rows) * 2
    return jax.shard_map(shards, mesh=mesh, in_specs=in_specs, out_specs=(maps, maps, maps), check_vma=False)
```

```python
import jax
import jax.numpy as jnp
from jax import lax
from jax.experimental import pallas as pl
from jax.experimental.pallas import tpu as pltpu
from jax.sharding import PartitionSpec as P


GROUPS = 32
TICKS = 2
IMAGES = 2
SIDE = 16
CELLS = SIDE * SIDE
HALF = CELLS // 2
C = 320
ROWS = IMAGES * CELLS
TAPS = 3 * C
F32 = jnp.float32
BF16 = jnp.bfloat16
PARCEL = (IMAGES, HALF, 2 * C)
HBM = pl.BlockSpec(memory_space=pltpu.HBM)
VMEM = pl.BlockSpec(memory_space=pltpu.VMEM)
WHOLE = jax.ShapeDtypeStruct((TICKS * ROWS, C), BF16)


def group_matrix(width):
    scale = 65536 // width + 1
    rows = lax.shift_right_logical(lax.broadcasted_iota(jnp.int32, (C, C), 0) * scale, 16)
    cols = lax.shift_right_logical(lax.broadcasted_iota(jnp.int32, (C, C), 1) * scale, 16)
    return jnp.where(rows == cols, 1.0, 0.0).astype(BF16)


def column_parts(values):
    return jnp.sum(values.reshape(CELLS // 8, 8, C), axis=0)


def group_means(parts, matrix, width):
    pieces = []
    for part in parts:
        high = part.astype(BF16).astype(F32)
        rest = part - high
        middle = rest.astype(BF16).astype(F32)
        pieces += [high, middle, rest - middle]
    stacked = jnp.concatenate(pieces, axis=0).astype(BF16)
    sums = jnp.dot(stacked, matrix, preferred_element_type=F32)
    weight = 1.0 / (width * CELLS)
    return [jnp.sum(sums[24 * i : 24 * (i + 1)], axis=0, keepdims=True) * weight for i in range(len(parts))]


def norm_all(loads, gains, betas, width):
    matrix = group_matrix(width)
    means = group_means([column_parts(load().astype(F32)) for load in loads], matrix, width)
    squares = []
    for load, mean in zip(loads, means):
        centred = load().astype(F32) - mean
        squares.append(column_parts(centred * centred))
    variances = group_means(squares, matrix, width)
    results = []
    for load, mean, variance, gain, beta in zip(loads, means, variances, gains, betas):
        half = ((load().astype(F32) - mean) * (lax.rsqrt(variance + 1e-05) * gain) + beta) * 0.5
        results.append((half * jnp.tanh(half) + half).astype(BF16))
    return results


def spread_rows(hidden):
    blank = jnp.zeros((SIDE, C), BF16)
    above = jnp.concatenate([blank, hidden[: CELLS - SIDE]], axis=0)
    below = jnp.concatenate([hidden[SIDE:], blank], axis=0)
    return jnp.concatenate([above, hidden, below], axis=1)


def gather_columns(sums):
    column = lax.broadcasted_iota(jnp.int32, (CELLS, C), 0) & (SIDE - 1)
    left = jnp.where(column > 0, pltpu.roll(sums[:, :C], 1, 0), 0.0)
    right = jnp.where(column < SIDE - 1, pltpu.roll(sums[:, 2 * C :], CELLS - 1, 0), 0.0)
    return left + sums[:, C : 2 * C] + right


def pack(value):
    return jnp.concatenate([value[:HALF], value[HALF:]], axis=1)


def unpack(value):
    return jnp.concatenate([value[:, :C], value[:, C:]], axis=0)


def begin(source, target, semaphore):
    copy = pltpu.make_async_copy(source, target, semaphore)
    copy.start()
    return copy


def image(index, base=0):
    return pl.ds(base + index * CELLS, CELLS)


def placed(value, spec):
    return pltpu.with_memory_space_constraint(value, pltpu.VMEM if spec is VMEM else pltpu.HBM)


def call(body, inputs, in_specs, outputs, scratch=(), aliases=None):
    held = [placed(value, spec) for value, spec in zip(inputs, in_specs)]
    return pl.pallas_call(
        body,
        out_shape=tuple(outputs),
        in_specs=list(in_specs),
        out_specs=tuple(HBM if isinstance(out, jax.ShapeDtypeStruct) else VMEM for out in outputs),
        scratch_shapes=list(scratch),
        input_output_aliases=aliases or {},
        compiler_params=pltpu.CompilerParams(vmem_limit_bytes=16 * 2**20),
    )(*held)


def enc_rest(current, gain, beta, bias, taps, wide, sums, send, ready=None):
    loads = [lambda i=i: current[image(i)] for i in range(IMAGES)]
    hidden = norm_all(loads, [gain[...]] * IMAGES, [beta[...]] * IMAGES, C // GROUPS)
    for i in range(IMAGES):
        wide[image(i)] = spread_rows(hidden[i])
    if ready is not None:
        ready()
    sums[...] = jnp.dot(wide[...], taps[...], preferred_element_type=F32)
    for i in range(IMAGES):
        total = current[image(i)].astype(F32) + gather_columns(sums[image(i)]) + bias[...]
        send[i] = pack(total.astype(BF16))


def enc_first(source, weight, enc_rows, later):
    count = len(later)

    def body(*refs):
        source, weight, bias, gain, beta = refs[:5]
        far = refs[5 : 5 + count]
        send, taps, bias_near, gain_near, beta_near = refs[5 + count : 10 + count]
        close = refs[10 + count : 10 + 2 * count]
        current, kernel, wide, sums, sems, later_sems = refs[10 + 2 * count :]
        first = [begin(source, current, sems.at[0])]
        first.append(begin(gain, gain_near, sems.at[1]))
        first.append(begin(beta, beta_near, sems.at[2]))
        first.append(begin(bias, bias_near, sems.at[3]))
        weights = [begin(weight.at[ky], kernel.at[ky], sems.at[4 + ky]) for ky in range(3)]
        fetched = [begin(far[k], close[k], later_sems.at[k]) for k in range(count)]
        for copy in first:
            copy.wait()

        def ready():
            for ky in range(3):
                weights[ky].wait()
                taps[pl.ds(ky * C, C)] = jnp.concatenate([kernel[ky, kx] for kx in range(3)], axis=1)

        enc_rest(current, gain_near, beta_near, bias_near, taps, wide, sums, send, ready)
        for copy in fetched:
            copy.wait()

    return call(
        body,
        (source, weight) + tuple(enc_rows) + tuple(later),
        [HBM] * (5 + count),
        [pltpu.VMEM(PARCEL, BF16), pltpu.VMEM((TAPS, TAPS), BF16)]
        + [pltpu.VMEM(row.shape, F32) for row in enc_rows]
        + [pltpu.VMEM(value.shape, value.dtype) for value in later],
        [
            pltpu.VMEM((ROWS, C), BF16),
            pltpu.VMEM((3, 3, C, C), BF16),
            pltpu.VMEM((ROWS, TAPS), BF16),
            pltpu.VMEM((ROWS, TAPS), F32),
            pltpu.SemaphoreType.DMA((7,)),
            pltpu.SemaphoreType.DMA((count,)),
        ],
    )


def write_maps(value, result, out, semaphores, base, slot):
    copies = []
    for i in range(IMAGES):
        result[image(i, slot * ROWS)] = unpack(value[i])
        copies.append(
            begin(result.at[image(i, slot * ROWS)], out.at[image(i, base)], semaphores.at[slot * IMAGES + i])
        )
    return copies


def enc_second(fresh, moved, taps, enc_rows, dec_sent):
    def body(fresh, moved, taps, bias, gain, beta, early, send, decoded, current, wide, sums, result, sems):
        copies = write_maps(early, result, decoded, sems, 0, 0)
        leading = lax.axis_index("section") == 0
        for i in range(IMAGES):
            current[image(i)] = jnp.where(leading, fresh[image(i)], unpack(moved[i]))
        enc_rest(current, gain, beta, bias, taps, wide, sums, send)
        for copy in copies:
            copy.wait()

    return call(
        body,
        (fresh, moved, taps) + tuple(enc_rows) + (dec_sent,),
        [VMEM] * 7,
        [pltpu.VMEM(PARCEL, BF16), WHOLE],
        [
            pltpu.VMEM((ROWS, C), BF16),
            pltpu.VMEM((ROWS, TAPS), BF16),
            pltpu.VMEM((ROWS, TAPS), F32),
            pltpu.VMEM((ROWS, C), BF16),
            pltpu.SemaphoreType.DMA((IMAGES,)),
        ],
    )


def multiply(wide, taps):
    return lax.dot_general(wide[...], taps[...], (((1,), (1,)), ((), ())), preferred_element_type=F32)


def dec_first(current, skips, kernel, dec_rows, enc_sent):
    def body(current, skips, kernel, bias, gain, beta, early, send, near, far, encoded, *scratch):
        wide, sums, result, sems = scratch
        taps = (near, far)
        copies = write_maps(early, result, encoded, sems, 0, 0)
        loads = [lambda m=m, i=i: m[image(i)] for m in (current, skips) for i in range(IMAGES)]
        gains = [gain[:, :C]] * IMAGES + [gain[:, C:]] * IMAGES
        betas = [beta[:, :C]] * IMAGES + [beta[:, C:]] * IMAGES
        hidden = norm_all(loads, gains, betas, 2 * C // GROUPS)
        for part in range(2):
            for i in range(IMAGES):
                wide[part, image(i)] = spread_rows(hidden[part * IMAGES + i])
            cut = slice(part * C, (part + 1) * C)
            taps[part][...] = jnp.concatenate([kernel[ky, :, cut] for ky in range(3)], axis=1)
        sums[...] = multiply(wide.at[0], near) + multiply(wide.at[1], far)
        for i in range(IMAGES):
            total = current[image(i)].astype(F32) + gather_columns(sums[image(i)]) + bias[...]
            send[i] = pack(total.astype(BF16))
        for copy in copies:
            copy.wait()

    return call(
        body,
        (current, skips, kernel) + tuple(dec_rows) + (enc_sent,),
        [VMEM] * 7,
        [pltpu.VMEM(PARCEL, BF16), pltpu.VMEM((TAPS, TAPS), BF16), pltpu.VMEM((TAPS, TAPS), BF16), WHOLE],
        [
            pltpu.VMEM((2, ROWS, TAPS), BF16),
            pltpu.VMEM((ROWS, TAPS), F32),
            pltpu.VMEM((ROWS, C), BF16),
            pltpu.SemaphoreType.DMA((IMAGES,)),
        ],
    )


def dec_skip(moved_enc, skips, taps, dec_rows, last_sent, encoded):
    def body(moved, skips, taps, bias, gain, beta, late, _, part, encoded, *scratch):
        result, skipped, wide, sums, sems = scratch
        copies = write_maps(late, result, encoded, sems, ROWS, 0)
        leading = lax.axis_index("section") == 0
        for i in range(IMAGES):
            skipped[image(i)] = jnp.where(leading, unpack(moved[i]), skips[image(i, ROWS)])
        loads = [lambda i=i: skipped[image(i)] for i in range(IMAGES)]
        hidden = norm_all(loads, [gain[:, C:]] * IMAGES, [beta[:, C:]] * IMAGES, 2 * C // GROUPS)
        for i in range(IMAGES):
            wide[image(i)] = spread_rows(hidden[i])
        sums[...] = multiply(wide, taps)
        for i in range(IMAGES):
            part[image(i)] = gather_columns(sums[image(i)]) + bias[...]
        for copy in copies:
            copy.wait()

    return call(
        body,
        (moved_enc, skips, taps) + tuple(dec_rows) + (last_sent, encoded),
        [VMEM] * 7 + [HBM],
        [pltpu.VMEM((ROWS, C), F32), WHOLE],
        [
            pltpu.VMEM((ROWS, C), BF16),
            pltpu.VMEM((ROWS, C), BF16),
            pltpu.VMEM((ROWS, TAPS), BF16),
            pltpu.VMEM((ROWS, TAPS), F32),
            pltpu.SemaphoreType.DMA((IMAGES,)),
        ],
        {7: 1},
    )


def dec_second(moved_enc, moved_dec, taps, part, dec_rows, decoded):
    def body(moved_enc, moved_dec, taps, part, gain, beta, _, out, *scratch):
        current, wide, sums, result, sems = scratch
        leading = lax.axis_index("section") == 0
        for i in range(IMAGES):
            current[image(i)] = unpack(jnp.where(leading, moved_enc[i], moved_dec[i]))
        loads = [lambda i=i: current[image(i)] for i in range(IMAGES)]
        hidden = norm_all(loads, [gain[:, :C]] * IMAGES, [beta[:, :C]] * IMAGES, 2 * C // GROUPS)
        for i in range(IMAGES):
            wide[image(i)] = spread_rows(hidden[i])
        sums[...] = multiply(wide, taps)
        copies = []
        for i in range(IMAGES):
            total = current[image(i)].astype(F32) + gather_columns(sums[image(i)]) + part[image(i)]
            result[image(i)] = total.astype(BF16)
            copies.append(begin(result.at[image(i)], out.at[image(i, ROWS)], sems.at[i]))
        for copy in copies:
            copy.wait()

    return call(
        body,
        (moved_enc, moved_dec, taps, part, dec_rows[1], dec_rows[2], decoded),
        [VMEM] * 6 + [HBM],
        [WHOLE],
        [
            pltpu.VMEM((ROWS, C), BF16),
            pltpu.VMEM((ROWS, TAPS), BF16),
            pltpu.VMEM((ROWS, TAPS), F32),
            pltpu.VMEM((ROWS, C), BF16),
            pltpu.SemaphoreType.DMA((IMAGES,)),
        ],
        {6: 0},
    )[0]


def queue_maps(turned, moved, last):
    def body(turned, moved, last, out, chosen, result, sems):
        shared = lax.axis_index("section") % 4 == 0
        for i in range(IMAGES):
            chosen[i] = jnp.where(shared, moved[i], turned[i])
        copies = write_maps(chosen, result, out, sems, 0, 0)
        copies += write_maps(last, result, out, sems, ROWS, 1)
        for copy in copies:
            copy.wait()

    return call(
        body,
        (turned, moved, last),
        [VMEM, VMEM, VMEM],
        [WHOLE],
        [
            pltpu.VMEM(PARCEL, BF16),
            pltpu.VMEM((2 * ROWS, C), BF16),
            pltpu.SemaphoreType.DMA((2 * IMAGES,)),
        ],
    )[0]


def shards(
    enc_in,
    dec_in,
    fresh,
    skip_queue,
    enc_weight,
    enc_bias,
    enc_gain,
    enc_beta,
    dec_weight,
    dec_bias,
    dec_gain,
    dec_beta,
):
    forward = [(s, (s + 1) % 8) for s in range(8)]
    mirror = [(s, 7 - s) for s in range(8)]
    relay = [(s, 8 - s) for s in range(1, 8) if s != 4]
    enc_kernel = enc_weight.reshape(3, 3, C, C)
    dec_kernel = jnp.transpose(dec_weight, (0, 1, 2, 4, 3)).reshape(3, TAPS, 2 * C)
    later = (
        dec_in.reshape(ROWS, C),
        skip_queue.reshape(TICKS * ROWS, C),
        dec_kernel,
        dec_bias,
        dec_gain,
        dec_beta,
        fresh.reshape(ROWS, C),
    )
    enc_sent, enc_taps, *held = enc_first(
        enc_in.reshape(ROWS, C), enc_kernel, (enc_bias, enc_gain, enc_beta), later
    )
    enc_rows, (dec_now, skips, dec_kernel), dec_rows, fresh_now = held[:3], held[3:6], held[6:9], held[9]
    moved_enc = lax.ppermute(enc_sent, "section", forward)
    dec_sent, dec_taps, skip_taps, encoded = dec_first(dec_now, skips, dec_kernel, dec_rows, enc_sent)
    moved_dec = lax.ppermute(dec_sent, "section", [pair for pair in forward if pair[1] != 0])
    turned = lax.ppermute(moved_enc, "section", relay)
    last_sent, decoded = enc_second(fresh_now, moved_enc, enc_taps, enc_rows, dec_sent)
    last = lax.ppermute(last_sent, "section", mirror)
    part, encoded = dec_skip(moved_enc, skips, skip_taps, dec_rows, last_sent, encoded)
    decoded = dec_second(moved_enc, moved_dec, dec_taps, part, dec_rows, decoded)
    queued = queue_maps(turned, moved_enc, last)
    shape = (TICKS * IMAGES, SIDE, SIDE, C)
    return encoded.reshape(shape), decoded.reshape(shape), queued.reshape(shape)


def solution(mesh):
    maps = P(("dp", "section"), None, None, None)
    rows = P("section", None)
    kernels = P("section", None, None, None, None)
    in_specs = (maps, maps, P("dp", None, None, None), maps) + (kernels, rows, rows, rows) * 2

    return jax.shard_map(shards, mesh=mesh, in_specs=in_specs, out_specs=(maps, maps, maps), check_vma=False)
```

```python
import jax
import jax.numpy as jnp
from jax import lax
from jax.experimental import pallas as pl
from jax.experimental.pallas import tpu as pltpu
from jax.sharding import PartitionSpec as P


GROUPS = 32
TICKS = 2
IMAGES = 2
SIDE = 16
CELLS = SIDE * SIDE
HALF = CELLS // 2
C = 320
ROWS = IMAGES * CELLS
TAPS = 3 * C
F32 = jnp.float32
BF16 = jnp.bfloat16
PARCEL = (IMAGES, HALF, 2 * C)
HBM = pl.BlockSpec(memory_space=pltpu.HBM)
VMEM = pl.BlockSpec(memory_space=pltpu.VMEM)
WHOLE = jax.ShapeDtypeStruct((TICKS * ROWS, C), BF16)


def group_matrix(width):
    scale = 65536 // width + 1
    rows = lax.shift_right_logical(lax.broadcasted_iota(jnp.int32, (C, C), 0) * scale, 16)
    cols = lax.shift_right_logical(lax.broadcasted_iota(jnp.int32, (C, C), 1) * scale, 16)
    return jnp.where(rows == cols, 1.0, 0.0).astype(BF16)


def column_parts(values):
    return jnp.sum(values.reshape(CELLS // 8, 8, C), axis=0)


def group_means(parts, matrix, width):
    pieces = []
    for part in parts:
        high = part.astype(BF16).astype(F32)
        rest = part - high
        middle = rest.astype(BF16).astype(F32)
        pieces += [high, middle, rest - middle]
    stacked = jnp.concatenate(pieces, axis=0).astype(BF16)
    sums = jnp.dot(stacked, matrix, preferred_element_type=F32)
    weight = 1.0 / (width * CELLS)
    return [jnp.sum(sums[24 * i : 24 * (i + 1)], axis=0, keepdims=True) * weight for i in range(len(parts))]


def norm_all(loads, gains, betas, width):
    matrix = group_matrix(width)
    means = group_means([column_parts(load().astype(F32)) for load in loads], matrix, width)
    squares = []
    for load, mean in zip(loads, means):
        centred = load().astype(F32) - mean
        squares.append(column_parts(centred * centred))
    variances = group_means(squares, matrix, width)
    results = []
    for load, mean, variance, gain, beta in zip(loads, means, variances, gains, betas):
        half = ((load().astype(F32) - mean) * (lax.rsqrt(variance + 1e-05) * gain) + beta) * 0.5
        results.append((half * jnp.tanh(half) + half).astype(BF16))
    return results


def spread_rows(hidden):
    blank = jnp.zeros((SIDE, C), BF16)
    above = jnp.concatenate([blank, hidden[: CELLS - SIDE]], axis=0)
    below = jnp.concatenate([hidden[SIDE:], blank], axis=0)
    return jnp.concatenate([above, hidden, below], axis=1)


def gather_columns(sums):
    column = lax.broadcasted_iota(jnp.int32, (CELLS, C), 0) & (SIDE - 1)
    left = jnp.where(column > 0, pltpu.roll(sums[:, :C], 1, 0), 0.0)
    right = jnp.where(column < SIDE - 1, pltpu.roll(sums[:, 2 * C :], CELLS - 1, 0), 0.0)
    return left + sums[:, C : 2 * C] + right


def pack(value):
    return jnp.concatenate([value[:HALF], value[HALF:]], axis=1)


def unpack(value):
    return jnp.concatenate([value[:, :C], value[:, C:]], axis=0)


def begin(source, target, semaphore):
    copy = pltpu.make_async_copy(source, target, semaphore)
    copy.start()
    return copy


def image(index, base=0):
    return pl.ds(base + index * CELLS, CELLS)


def placed(value, spec):
    return pltpu.with_memory_space_constraint(value, pltpu.VMEM if spec is VMEM else pltpu.HBM)


def call(body, inputs, in_specs, outputs, scratch=(), aliases=None):
    held = [placed(value, spec) for value, spec in zip(inputs, in_specs)]
    return pl.pallas_call(
        body,
        out_shape=tuple(outputs),
        in_specs=list(in_specs),
        out_specs=tuple(HBM if isinstance(out, jax.ShapeDtypeStruct) else VMEM for out in outputs),
        scratch_shapes=list(scratch),
        input_output_aliases=aliases or {},
        compiler_params=pltpu.CompilerParams(vmem_limit_bytes=24 * 2**20),
    )(*held)


def enc_rest(current, gain, beta, bias, taps, wide, sums, send, ready=None):
    loads = [lambda i=i: current[image(i)] for i in range(IMAGES)]
    hidden = norm_all(loads, [gain[...]] * IMAGES, [beta[...]] * IMAGES, C // GROUPS)
    for i in range(IMAGES):
        wide[image(i)] = spread_rows(hidden[i])
    if ready is not None:
        ready()
    sums[...] = jnp.dot(wide[...], taps[...], preferred_element_type=F32)
    for i in range(IMAGES):
        total = current[image(i)].astype(F32) + gather_columns(sums[image(i)]) + bias[...]
        send[i] = pack(total.astype(BF16))


def enc_first(source, weight, enc_rows, later):
    count = len(later)

    def body(*refs):
        source, weight, bias, gain, beta = refs[:5]
        far = refs[5 : 5 + count]
        send, taps, bias_near, gain_near, beta_near = refs[5 + count : 10 + count]
        close = refs[10 + count : 10 + 2 * count]
        current, kernel, wide, sums, sems, later_sems = refs[10 + 2 * count :]
        first = [begin(source, current, sems.at[0])]
        first.append(begin(gain, gain_near, sems.at[1]))
        first.append(begin(beta, beta_near, sems.at[2]))
        first.append(begin(bias, bias_near, sems.at[3]))
        weights = [begin(weight.at[ky], kernel.at[ky], sems.at[4 + ky]) for ky in range(3)]
        fetched = []
        for copy in first:
            copy.wait()

        def ready():
            for copy in weights:
                copy.wait()
            fetched.extend(begin(far[k], close[k], later_sems.at[k]) for k in range(count))
            for ky in range(3):
                taps[pl.ds(ky * C, C)] = jnp.concatenate([kernel[ky, kx] for kx in range(3)], axis=1)

        enc_rest(current, gain_near, beta_near, bias_near, taps, wide, sums, send, ready)
        for copy in fetched:
            copy.wait()

    return call(
        body,
        (source, weight) + tuple(enc_rows) + tuple(later),
        [HBM] * (5 + count),
        [pltpu.VMEM(PARCEL, BF16), pltpu.VMEM((TAPS, TAPS), BF16)]
        + [pltpu.VMEM(row.shape, F32) for row in enc_rows]
        + [pltpu.VMEM(value.shape, value.dtype) for value in later],
        [
            pltpu.VMEM((ROWS, C), BF16),
            pltpu.VMEM((3, 3, C, C), BF16),
            pltpu.VMEM((ROWS, TAPS), BF16),
            pltpu.VMEM((ROWS, TAPS), F32),
            pltpu.SemaphoreType.DMA((7,)),
            pltpu.SemaphoreType.DMA((count,)),
        ],
    )


def write_maps(value, result, out, semaphores, base, slot):
    copies = []
    for i in range(IMAGES):
        result[image(i, slot * ROWS)] = unpack(value[i])
        copies.append(
            begin(result.at[image(i, slot * ROWS)], out.at[image(i, base)], semaphores.at[slot * IMAGES + i])
        )
    return copies


def enc_second(fresh, moved, taps, enc_rows, dec_sent):
    def body(fresh, moved, taps, bias, gain, beta, early, send, decoded, current, wide, sums, result, sems):
        copies = write_maps(early, result, decoded, sems, 0, 0)
        leading = lax.axis_index("section") == 0
        for i in range(IMAGES):
            current[image(i)] = jnp.where(leading, fresh[image(i)], unpack(moved[i]))
        enc_rest(current, gain, beta, bias, taps, wide, sums, send)
        for copy in copies:
            copy.wait()

    return call(
        body,
        (fresh, moved, taps) + tuple(enc_rows) + (dec_sent,),
        [VMEM] * 7,
        [pltpu.VMEM(PARCEL, BF16), WHOLE],
        [
            pltpu.VMEM((ROWS, C), BF16),
            pltpu.VMEM((ROWS, TAPS), BF16),
            pltpu.VMEM((ROWS, TAPS), F32),
            pltpu.VMEM((ROWS, C), BF16),
            pltpu.SemaphoreType.DMA((IMAGES,)),
        ],
    )


def multiply(wide, taps):
    return lax.dot_general(wide[...], taps[...], (((1,), (1,)), ((), ())), preferred_element_type=F32)


def dec_first(current, skips, weight, dec_rows, enc_sent):
    def body(current, skips, weight, bias, gain, beta, early, send, near, far, part, encoded, *scratch):
        kernel, wide, sums, ahead, result, sems = scratch
        weights = [begin(weight.at[ky], kernel.at[ky], sems.at[IMAGES + ky]) for ky in range(3)]
        copies = write_maps(early, result, encoded, sems, 0, 0)
        starts = ((current, 0), (skips, 0), (skips, ROWS))
        loads = [lambda m=m, i=i, base=base: m[image(i, base)] for m, base in starts for i in range(IMAGES)]
        gains = [gain[:, :C]] * IMAGES + [gain[:, C:]] * (2 * IMAGES)
        betas = [beta[:, :C]] * IMAGES + [beta[:, C:]] * (2 * IMAGES)
        hidden = norm_all(loads, gains, betas, 2 * C // GROUPS)
        for source in range(3):
            for i in range(IMAGES):
                wide[source, image(i)] = spread_rows(hidden[source * IMAGES + i])
        for copy in weights:
            copy.wait()
        for half, taps in enumerate((near, far)):
            cut = slice(half * C, (half + 1) * C)
            taps[...] = jnp.concatenate([kernel[ky, :, cut] for ky in range(3)], axis=1)
        sums[...] = multiply(wide.at[0], near) + multiply(wide.at[1], far)
        for i in range(IMAGES):
            total = current[image(i)].astype(F32) + gather_columns(sums[image(i)]) + bias[...]
            send[i] = pack(total.astype(BF16))
        ahead[...] = multiply(wide.at[2], far)
        for i in range(IMAGES):
            part[image(i)] = gather_columns(ahead[image(i)]) + bias[...]
        for copy in copies:
            copy.wait()

    return call(
        body,
        (current, skips, weight) + tuple(dec_rows) + (enc_sent,),
        [VMEM, VMEM, HBM] + [VMEM] * 4,
        [
            pltpu.VMEM(PARCEL, BF16),
            pltpu.VMEM((TAPS, TAPS), BF16),
            pltpu.VMEM((TAPS, TAPS), BF16),
            pltpu.VMEM((ROWS, C), F32),
            WHOLE,
        ],
        [
            pltpu.VMEM((3, TAPS, 2 * C), BF16),
            pltpu.VMEM((3, ROWS, TAPS), BF16),
            pltpu.VMEM((ROWS, TAPS), F32),
            pltpu.VMEM((ROWS, TAPS), F32),
            pltpu.VMEM((ROWS, C), BF16),
            pltpu.SemaphoreType.DMA((IMAGES + 3,)),
        ],
    )


def dec_second(moved_enc, moved_dec, near, far, part, dec_rows, last_sent, encoded, decoded):
    def body(moved_enc, moved_dec, near, far, part, bias, gain, beta, late, _, __, encoded, decoded, *scratch):
        current, wide, sums, skip_part, written, result, sems = scratch
        copies = write_maps(late, written, encoded, sems, ROWS, 0)
        leading = lax.axis_index("section") == 0
        for i in range(IMAGES):
            current[image(i)] = unpack(jnp.where(leading, moved_enc[i], moved_dec[i]))
        loads = [lambda i=i: current[image(i)] for i in range(IMAGES)]

        def product(half, taps):
            cut = slice(half * C, (half + 1) * C)
            hidden = norm_all(loads, [gain[:, cut]] * IMAGES, [beta[:, cut]] * IMAGES, 2 * C // GROUPS)
            for i in range(IMAGES):
                wide[image(i)] = spread_rows(hidden[i])
            sums[...] = multiply(wide, taps)

        @pl.when(leading)
        def _():
            product(1, far)
            for i in range(IMAGES):
                skip_part[image(i)] = gather_columns(sums[image(i)]) + bias[...]

        @pl.when(jnp.logical_not(leading))
        def _():
            skip_part[...] = part[...]

        product(0, near)
        for i in range(IMAGES):
            total = current[image(i)].astype(F32) + gather_columns(sums[image(i)]) + skip_part[image(i)]
            result[image(i)] = total.astype(BF16)
            copies.append(begin(result.at[image(i)], decoded.at[image(i, ROWS)], sems.at[IMAGES + i]))
        for copy in copies:
            copy.wait()

    return call(
        body,
        (moved_enc, moved_dec, near, far, part) + tuple(dec_rows) + (last_sent, encoded, decoded),
        [VMEM] * 9 + [HBM, HBM],
        [WHOLE, WHOLE],
        [
            pltpu.VMEM((ROWS, C), BF16),
            pltpu.VMEM((ROWS, TAPS), BF16),
            pltpu.VMEM((ROWS, TAPS), F32),
            pltpu.VMEM((ROWS, C), F32),
            pltpu.VMEM((ROWS, C), BF16),
            pltpu.VMEM((ROWS, C), BF16),
            pltpu.SemaphoreType.DMA((2 * IMAGES,)),
        ],
        {9: 0, 10: 1},
    )


def queue_maps(direct, turned, moved, last):
    def body(direct, turned, moved, last, out, chosen, result, sems):
        shared = lax.axis_index("section") % 4 == 0
        first = lax.axis_index("dp") % 2 == 0
        for i in range(IMAGES):
            chosen[i] = jnp.where(shared, moved[i], jnp.where(first, direct[i], turned[i]))
        copies = write_maps(chosen, result, out, sems, 0, 0)
        copies += write_maps(last, result, out, sems, ROWS, 1)
        for copy in copies:
            copy.wait()

    return call(
        body,
        (direct, turned, moved, last),
        [VMEM, VMEM, VMEM, VMEM],
        [WHOLE],
        [
            pltpu.VMEM(PARCEL, BF16),
            pltpu.VMEM((2 * ROWS, C), BF16),
            pltpu.SemaphoreType.DMA((2 * IMAGES,)),
        ],
    )[0]


def shards(
    enc_in,
    dec_in,
    fresh,
    skip_queue,
    enc_weight,
    enc_bias,
    enc_gain,
    enc_beta,
    dec_weight,
    dec_bias,
    dec_gain,
    dec_beta,
):
    forward = [(s, (s + 1) % 8) for s in range(8)]
    mirror = [(s, 7 - s) for s in range(8)]
    groups = lax.axis_size("dp")
    direct = [(groups * s + g, groups * (7 - s) + g) for g in range(0, groups, 2) for s in range(8) if s % 4 != 3]
    relay = [(groups * s + g, groups * (8 - s) + g) for g in range(1, groups, 2) for s in range(8) if s % 4]
    enc_kernel = enc_weight.reshape(3, 3, C, C)
    dec_kernel = jnp.transpose(dec_weight, (0, 1, 2, 4, 3)).reshape(3, TAPS, 2 * C)
    later = (
        dec_in.reshape(ROWS, C),
        skip_queue.reshape(TICKS * ROWS, C),
        dec_bias,
        dec_gain,
        dec_beta,
        fresh.reshape(ROWS, C),
    )
    enc_sent, enc_taps, *held = enc_first(
        enc_in.reshape(ROWS, C), enc_kernel, (enc_bias, enc_gain, enc_beta), later
    )
    enc_rows, (dec_now, skips), dec_rows, fresh_now = held[:3], held[3:5], held[5:8], held[8]
    moved_enc = lax.ppermute(enc_sent, "section", forward)
    turned_direct = lax.ppermute(enc_sent, ("section", "dp"), direct)
    dec_sent, near, far, part, encoded = dec_first(dec_now, skips, dec_kernel, dec_rows, enc_sent)
    turned = lax.ppermute(moved_enc, ("section", "dp"), relay)
    moved_dec = lax.ppermute(dec_sent, "section", [pair for pair in forward if pair[1] != 0])
    last_sent, decoded = enc_second(fresh_now, moved_enc, enc_taps, enc_rows, dec_sent)
    last = lax.ppermute(last_sent, "section", mirror)
    encoded, decoded = dec_second(
        moved_enc, moved_dec, near, far, part, dec_rows, last_sent, encoded, decoded
    )
    queued = queue_maps(turned_direct, turned, moved_enc, last)
    shape = (TICKS * IMAGES, SIDE, SIDE, C)
    return encoded.reshape(shape), decoded.reshape(shape), queued.reshape(shape)


def solution(mesh):
    maps = P(("dp", "section"), None, None, None)
    rows = P("section", None)
    kernels = P("section", None, None, None, None)
    in_specs = (maps, maps, P("dp", None, None, None), maps) + (kernels, rows, rows, rows) * 2

    return jax.shard_map(shards, mesh=mesh, in_specs=in_specs, out_specs=(maps, maps, maps), check_vma=False)
```

```python
import jax
import jax.numpy as jnp
from jax import lax
from jax.experimental import pallas as pl
from jax.experimental.pallas import tpu as pltpu
from jax.sharding import PartitionSpec as P


GROUPS = 32
TICKS = 2
IMAGES = 2
SIDE = 16
CELLS = SIDE * SIDE
HALF = CELLS // 2
C = 320
ROWS = IMAGES * CELLS
TAPS = 3 * C
F32 = jnp.float32
BF16 = jnp.bfloat16
PARCEL = (IMAGES, HALF, 2 * C)
HBM = pl.BlockSpec(memory_space=pltpu.HBM)
VMEM = pl.BlockSpec(memory_space=pltpu.VMEM)
WHOLE = jax.ShapeDtypeStruct((TICKS * ROWS, C), BF16)


def group_matrix(width):
    scale = 65536 // width + 1
    rows = lax.shift_right_logical(lax.broadcasted_iota(jnp.int32, (C, C), 0) * scale, 16)
    cols = lax.shift_right_logical(lax.broadcasted_iota(jnp.int32, (C, C), 1) * scale, 16)
    return jnp.where(rows == cols, 1.0, 0.0).astype(BF16)


def column_parts(values):
    return jnp.sum(values.reshape(CELLS // 8, 8, C), axis=0)


def group_means(parts, matrix, width):
    pieces = []
    for part in parts:
        high = part.astype(BF16).astype(F32)
        rest = part - high
        middle = rest.astype(BF16).astype(F32)
        pieces += [high, middle, rest - middle]
    stacked = jnp.concatenate(pieces, axis=0).astype(BF16)
    sums = jnp.dot(stacked, matrix, preferred_element_type=F32)
    weight = 1.0 / (width * CELLS)
    return [jnp.sum(sums[24 * i : 24 * (i + 1)], axis=0, keepdims=True) * weight for i in range(len(parts))]


def norm_all(loads, gains, betas, width):
    matrix = group_matrix(width)
    means = group_means([column_parts(load().astype(F32)) for load in loads], matrix, width)
    squares = []
    for load, mean in zip(loads, means):
        centred = load().astype(F32) - mean
        squares.append(column_parts(centred * centred))
    variances = group_means(squares, matrix, width)
    results = []
    for load, mean, variance, gain, beta in zip(loads, means, variances, gains, betas):
        half = ((load().astype(F32) - mean) * (lax.rsqrt(variance + 1e-05) * gain) + beta) * 0.5
        results.append((half * jnp.tanh(half) + half).astype(BF16))
    return results


def spread_rows(hidden):
    blank = jnp.zeros((SIDE, C), BF16)
    above = jnp.concatenate([blank, hidden[: CELLS - SIDE]], axis=0)
    below = jnp.concatenate([hidden[SIDE:], blank], axis=0)
    return jnp.concatenate([above, hidden, below], axis=1)


def gather_columns(sums):
    column = lax.broadcasted_iota(jnp.int32, (CELLS, C), 0) & (SIDE - 1)
    left = jnp.where(column > 0, pltpu.roll(sums[:, :C], 1, 0), 0.0)
    right = jnp.where(column < SIDE - 1, pltpu.roll(sums[:, 2 * C :], CELLS - 1, 0), 0.0)
    return left + sums[:, C : 2 * C] + right


def pack(value):
    return jnp.concatenate([value[:HALF], value[HALF:]], axis=1)


def unpack(value):
    return jnp.concatenate([value[:, :C], value[:, C:]], axis=0)


def begin(source, target, semaphore):
    copy = pltpu.make_async_copy(source, target, semaphore)
    copy.start()
    return copy


def image(index, base=0):
    return pl.ds(base + index * CELLS, CELLS)


def placed(value, spec):
    return pltpu.with_memory_space_constraint(value, pltpu.VMEM if spec is VMEM else pltpu.HBM)


def call(body, inputs, in_specs, outputs, scratch=(), aliases=None):
    held = [placed(value, spec) for value, spec in zip(inputs, in_specs)]
    return pl.pallas_call(
        body,
        out_shape=tuple(outputs),
        in_specs=list(in_specs),
        out_specs=tuple(HBM if isinstance(out, jax.ShapeDtypeStruct) else VMEM for out in outputs),
        scratch_shapes=list(scratch),
        input_output_aliases=aliases or {},
        compiler_params=pltpu.CompilerParams(vmem_limit_bytes=24 * 2**20),
    )(*held)


def enc_rest(current, gain, beta, bias, taps, wide, sums, send, ready=None):
    loads = [lambda i=i: current[image(i)] for i in range(IMAGES)]
    hidden = norm_all(loads, [gain[...]] * IMAGES, [beta[...]] * IMAGES, C // GROUPS)
    for i in range(IMAGES):
        wide[image(i)] = spread_rows(hidden[i])
    if ready is not None:
        ready()
    sums[...] = jnp.dot(wide[...], taps[...], preferred_element_type=F32)
    for i in range(IMAGES):
        total = current[image(i)].astype(F32) + gather_columns(sums[image(i)]) + bias[...]
        send[i] = pack(total.astype(BF16))


def enc_first(source, weight, enc_rows, later):
    count = len(later)

    def body(*refs):
        source, weight, bias, gain, beta = refs[:5]
        far = refs[5 : 5 + count]
        send, taps, bias_near, gain_near, beta_near = refs[5 + count : 10 + count]
        close = refs[10 + count : 10 + 2 * count]
        current, kernel, wide, sums, sems, later_sems = refs[10 + 2 * count :]
        first = [begin(source, current, sems.at[0])]
        first.append(begin(gain, gain_near, sems.at[1]))
        first.append(begin(beta, beta_near, sems.at[2]))
        first.append(begin(bias, bias_near, sems.at[3]))
        weights = [begin(weight.at[ky], kernel.at[ky], sems.at[4 + ky]) for ky in range(3)]
        fetched = []
        for copy in first:
            copy.wait()

        def ready():
            for copy in weights:
                copy.wait()
            fetched.extend(begin(far[k], close[k], later_sems.at[k]) for k in range(count))
            for ky in range(3):
                taps[pl.ds(ky * C, C)] = jnp.concatenate([kernel[ky, kx] for kx in range(3)], axis=1)

        enc_rest(current, gain_near, beta_near, bias_near, taps, wide, sums, send, ready)
        for copy in fetched:
            copy.wait()

    return call(
        body,
        (source, weight) + tuple(enc_rows) + tuple(later),
        [HBM] * (5 + count),
        [pltpu.VMEM(PARCEL, BF16), pltpu.VMEM((TAPS, TAPS), BF16)]
        + [pltpu.VMEM(row.shape, F32) for row in enc_rows]
        + [pltpu.VMEM(value.shape, value.dtype) for value in later],
        [
            pltpu.VMEM((ROWS, C), BF16),
            pltpu.VMEM((3, 3, C, C), BF16),
            pltpu.VMEM((ROWS, TAPS), BF16),
            pltpu.VMEM((ROWS, TAPS), F32),
            pltpu.SemaphoreType.DMA((7,)),
            pltpu.SemaphoreType.DMA((count,)),
        ],
    )


def write_maps(value, result, out, semaphores, base, slot):
    copies = []
    for i in range(IMAGES):
        result[image(i, slot * ROWS)] = unpack(value[i])
        copies.append(
            begin(result.at[image(i, slot * ROWS)], out.at[image(i, base)], semaphores.at[slot * IMAGES + i])
        )
    return copies


def enc_second(fresh, moved, taps, enc_rows, dec_sent):
    def body(fresh, moved, taps, bias, gain, beta, early, send, decoded, current, wide, sums, result, sems):
        copies = write_maps(early, result, decoded, sems, 0, 0)
        leading = lax.axis_index("section") == 0
        for i in range(IMAGES):
            current[image(i)] = jnp.where(leading, fresh[image(i)], unpack(moved[i]))
        enc_rest(current, gain, beta, bias, taps, wide, sums, send)
        for copy in copies:
            copy.wait()

    return call(
        body,
        (fresh, moved, taps) + tuple(enc_rows) + (dec_sent,),
        [VMEM] * 7,
        [pltpu.VMEM(PARCEL, BF16), WHOLE],
        [
            pltpu.VMEM((ROWS, C), BF16),
            pltpu.VMEM((ROWS, TAPS), BF16),
            pltpu.VMEM((ROWS, TAPS), F32),
            pltpu.VMEM((ROWS, C), BF16),
            pltpu.SemaphoreType.DMA((IMAGES,)),
        ],
    )


def multiply(wide, taps):
    return lax.dot_general(wide[...], taps[...], (((1,), (1,)), ((), ())), preferred_element_type=F32)


def dec_first(current, skips, weight, dec_rows, enc_sent):
    def body(current, skips, weight, bias, gain, beta, early, send, near, far, encoded, *scratch):
        kernel, wide, sums, result, sems = scratch
        weights = [begin(weight.at[ky], kernel.at[ky], sems.at[IMAGES + ky]) for ky in range(3)]
        copies = write_maps(early, result, encoded, sems, 0, 0)
        starts = ((current, 0), (skips, 0))
        loads = [lambda m=m, i=i, base=base: m[image(i, base)] for m, base in starts for i in range(IMAGES)]
        gains = [gain[:, :C]] * IMAGES + [gain[:, C:]] * IMAGES
        betas = [beta[:, :C]] * IMAGES + [beta[:, C:]] * IMAGES
        hidden = norm_all(loads, gains, betas, 2 * C // GROUPS)
        for source in range(2):
            for i in range(IMAGES):
                wide[source, image(i)] = spread_rows(hidden[source * IMAGES + i])
        for copy in weights:
            copy.wait()
        for half, taps in enumerate((near, far)):
            cut = slice(half * C, (half + 1) * C)
            taps[...] = jnp.concatenate([kernel[ky, :, cut] for ky in range(3)], axis=1)
        sums[...] = multiply(wide.at[0], near) + multiply(wide.at[1], far)
        for i in range(IMAGES):
            total = current[image(i)].astype(F32) + gather_columns(sums[image(i)]) + bias[...]
            send[i] = pack(total.astype(BF16))
        for copy in copies:
            copy.wait()

    return call(
        body,
        (current, skips, weight) + tuple(dec_rows) + (enc_sent,),
        [VMEM, VMEM, HBM] + [VMEM] * 4,
        [
            pltpu.VMEM(PARCEL, BF16),
            pltpu.VMEM((TAPS, TAPS), BF16),
            pltpu.VMEM((TAPS, TAPS), BF16),
            WHOLE,
        ],
        [
            pltpu.VMEM((3, TAPS, 2 * C), BF16),
            pltpu.VMEM((2, ROWS, TAPS), BF16),
            pltpu.VMEM((ROWS, TAPS), F32),
            pltpu.VMEM((ROWS, C), BF16),
            pltpu.SemaphoreType.DMA((IMAGES + 3,)),
        ],
    )


def dec_skip(moved_enc, skips, taps, dec_rows, last_sent, encoded):
    def body(moved, skips, taps, bias, gain, beta, late, _, part, encoded, *scratch):
        result, skipped, wide, sums, sems = scratch
        copies = write_maps(late, result, encoded, sems, ROWS, 0)
        leading = lax.axis_index("section") == 0
        for i in range(IMAGES):
            skipped[image(i)] = jnp.where(leading, unpack(moved[i]), skips[image(i, ROWS)])
        loads = [lambda i=i: skipped[image(i)] for i in range(IMAGES)]
        hidden = norm_all(loads, [gain[:, C:]] * IMAGES, [beta[:, C:]] * IMAGES, 2 * C // GROUPS)
        for i in range(IMAGES):
            wide[image(i)] = spread_rows(hidden[i])
        sums[...] = multiply(wide, taps)
        for i in range(IMAGES):
            part[image(i)] = gather_columns(sums[image(i)]) + bias[...]
        for copy in copies:
            copy.wait()

    return call(
        body,
        (moved_enc, skips, taps) + tuple(dec_rows) + (last_sent, encoded),
        [VMEM] * 7 + [HBM],
        [pltpu.VMEM((ROWS, C), F32), WHOLE],
        [
            pltpu.VMEM((ROWS, C), BF16),
            pltpu.VMEM((ROWS, C), BF16),
            pltpu.VMEM((ROWS, TAPS), BF16),
            pltpu.VMEM((ROWS, TAPS), F32),
            pltpu.SemaphoreType.DMA((IMAGES,)),
        ],
        {7: 1},
    )


def dec_second(moved_enc, moved_dec, taps, part, dec_rows, decoded):
    def body(moved_enc, moved_dec, taps, part, gain, beta, _, out, *scratch):
        current, wide, sums, result, sems = scratch
        leading = lax.axis_index("section") == 0
        for i in range(IMAGES):
            current[image(i)] = unpack(jnp.where(leading, moved_enc[i], moved_dec[i]))
        loads = [lambda i=i: current[image(i)] for i in range(IMAGES)]
        hidden = norm_all(loads, [gain[:, :C]] * IMAGES, [beta[:, :C]] * IMAGES, 2 * C // GROUPS)
        for i in range(IMAGES):
            wide[image(i)] = spread_rows(hidden[i])
        sums[...] = multiply(wide, taps)
        copies = []
        for i in range(IMAGES):
            total = current[image(i)].astype(F32) + gather_columns(sums[image(i)]) + part[image(i)]
            result[image(i)] = total.astype(BF16)
            copies.append(begin(result.at[image(i)], out.at[image(i, ROWS)], sems.at[i]))
        for copy in copies:
            copy.wait()

    return call(
        body,
        (moved_enc, moved_dec, taps, part, dec_rows[1], dec_rows[2], decoded),
        [VMEM] * 6 + [HBM],
        [WHOLE],
        [
            pltpu.VMEM((ROWS, C), BF16),
            pltpu.VMEM((ROWS, TAPS), BF16),
            pltpu.VMEM((ROWS, TAPS), F32),
            pltpu.VMEM((ROWS, C), BF16),
            pltpu.SemaphoreType.DMA((IMAGES,)),
        ],
        {6: 0},
    )[0]


def queue_maps(direct, turned, moved, last):
    def body(direct, turned, moved, last, out, chosen, result, sems):
        shared = lax.axis_index("section") % 4 == 0
        first = lax.axis_index("dp") % 2 == 0
        for i in range(IMAGES):
            chosen[i] = jnp.where(shared, moved[i], jnp.where(first, direct[i], turned[i]))
        copies = write_maps(chosen, result, out, sems, 0, 0)
        copies += write_maps(last, result, out, sems, ROWS, 1)
        for copy in copies:
            copy.wait()

    return call(
        body,
        (direct, turned, moved, last),
        [VMEM, VMEM, VMEM, VMEM],
        [WHOLE],
        [
            pltpu.VMEM(PARCEL, BF16),
            pltpu.VMEM((2 * ROWS, C), BF16),
            pltpu.SemaphoreType.DMA((2 * IMAGES,)),
        ],
    )[0]


def shards(
    enc_in,
    dec_in,
    fresh,
    skip_queue,
    enc_weight,
    enc_bias,
    enc_gain,
    enc_beta,
    dec_weight,
    dec_bias,
    dec_gain,
    dec_beta,
):
    forward = [(s, (s + 1) % 8) for s in range(8)]
    mirror = [(s, 7 - s) for s in range(8)]
    groups = lax.axis_size("dp")
    direct = [(groups * s + g, groups * (7 - s) + g) for g in range(0, groups, 2) for s in range(8) if s % 4 != 3]
    relay = [(groups * s + g, groups * (8 - s) + g) for g in range(1, groups, 2) for s in range(8) if s % 4]
    enc_kernel = enc_weight.reshape(3, 3, C, C)
    dec_kernel = jnp.transpose(dec_weight, (0, 1, 2, 4, 3)).reshape(3, TAPS, 2 * C)
    later = (
        dec_in.reshape(ROWS, C),
        skip_queue.reshape(TICKS * ROWS, C),
        dec_bias,
        dec_gain,
        dec_beta,
        fresh.reshape(ROWS, C),
    )
    enc_sent, enc_taps, *held = enc_first(
        enc_in.reshape(ROWS, C), enc_kernel, (enc_bias, enc_gain, enc_beta), later
    )
    enc_rows, (dec_now, skips), dec_rows, fresh_now = held[:3], held[3:5], held[5:8], held[8]
    moved_enc = lax.ppermute(enc_sent, "section", forward)
    turned_direct = lax.ppermute(enc_sent, ("section", "dp"), direct)
    dec_sent, near, far, encoded = dec_first(dec_now, skips, dec_kernel, dec_rows, enc_sent)
    turned = lax.ppermute(moved_enc, ("section", "dp"), relay)
    moved_dec = lax.ppermute(dec_sent, "section", [pair for pair in forward if pair[1] != 0])
    last_sent, decoded = enc_second(fresh_now, moved_enc, enc_taps, enc_rows, dec_sent)
    last = lax.ppermute(last_sent, "section", mirror)
    part, encoded = dec_skip(moved_enc, skips, far, dec_rows, last_sent, encoded)
    decoded = dec_second(moved_enc, moved_dec, near, part, dec_rows, decoded)
    queued = queue_maps(turned_direct, turned, moved_enc, last)
    shape = (TICKS * IMAGES, SIDE, SIDE, C)
    return encoded.reshape(shape), decoded.reshape(shape), queued.reshape(shape)


def solution(mesh):
    maps = P(("dp", "section"), None, None, None)
    rows = P("section", None)
    kernels = P("section", None, None, None, None)
    in_specs = (maps, maps, P("dp", None, None, None), maps) + (kernels, rows, rows, rows) * 2

    return jax.shard_map(shards, mesh=mesh, in_specs=in_specs, out_specs=(maps, maps, maps), check_vma=False)
```
